512 devices in a mesh: row: 32 (over y_lo, x, core), col: 16 (over z, y_hi).
Axes of the slice: x: 4, y: 8 (y_hi: 2, y_lo: 4; y = y_hi * 4 + y_lo), z: 8, core: 2. Of those that a mesh axis runs over, the one named last changes fastest.
Arguments:
- features: bfloat16 [98304, 256], P(('row', 'col')), may hold values from -6 to 6
- weight: bfloat16 [256, 256], replicated, may hold values from -0.375 to 0.375
- tiles: bfloat16 [32, 16, 256, 64, 128], P('row', 'col'), may hold values from -0.0546875 to 0.0546875
- tile_rows: int32 [32, 16, 512], P('row', 'col'), may hold values from 0 to 47
- tile_cols: int32 [32, 16, 512], P('row', 'col'), may hold values from 0 to 95
- counts: int32 [32, 16], P('row', 'col'), may hold values from 128 to 512, as said below
Outputs:
- output: bfloat16 [98304, 256], P(('row', 'col'))
The draws below stay inside these ranges and needn't reach their ends.
Inputs may be any that keep to these rules, and one draw needn't show every extreme that they name: `counts`: some grid cell has exactly 512 live slots.
All inputs are finite; a program needn't handle non-finite values.
Results may differ from the reference program's by a relative error of at most 0.0049.
Values may be sent and summed in bfloat16 or wider, within the bound.
No kernel may reach another device: no remote copies, remote signals or barrier semaphores. Data moves between devices by JAX's collectives and lax.ppermute only.
A program may use at most 64 MiB of HBM per device.

```python
import jax
import jax.numpy as jnp
from jax import lax

F = 256
TILE = 64
S = 192
TPD = 512
NODES = 98304
ROWT = 48
COLT = 96
N_ROW = 32
N_COL = 16


def draw_counts(key, part):
    first_key, second_key = jax.random.split(jax.random.fold_in(key, 17))
    values = jax.random.randint(first_key, (N_ROW * N_COL,), TPD // 4, TPD + 1, dtype=jnp.int32)
    location = jax.random.randint(second_key, (), 0, N_ROW * N_COL, dtype=jnp.int32)
    values = values.at[location].set(TPD)
    return values.reshape(N_ROW, N_COL)


def touch_ends(drawn, own_key, low, top_value):
    dims = drawn.shape
    spot = [jax.random.randint(jax.random.fold_in(own_key, axis), (), 0, dims[axis]) for axis in range(len(dims))]
    drawn = drawn.at[tuple(spot)].set(low)
    longest = dims.index(max(dims))
    spot[longest] = (spot[longest] + 1) % dims[longest]
    return drawn.at[tuple(spot)].set(top_value)


def shard_levels(rng, extent, shards, smallest, largest):
    level, own = 1.0, jax.random.fold_in(rng, 6)
    for position, shards_of in shards:
        steps = jnp.exp(jax.random.uniform(jax.random.fold_in(own, position), (shards_of,), jnp.float32, smallest / len(shards), largest / len(shards)))
        level = level * jnp.repeat(steps, extent[position] // shards_of).reshape([-1 if axis == position else 1 for axis in range(len(extent))])
    return level


def bell_draw(own_key, shape, deviation, bound, cuts=(), held_as=jnp.bfloat16):
    level = shard_levels(own_key, shape, cuts, -0.22, 0.18) if cuts else 1.0
    values = jax.random.normal(own_key, shape, jnp.float32) * deviation * level
    return jnp.minimum(jnp.maximum(values, -bound), bound).astype(held_as)


def setup_inputs(seed: int = 0) -> dict:
    streams_of = jax.random.split(jax.random.key(seed), 7)
    return {
        "features": bell_draw(streams_of[0], (NODES, F), 1.0, 6.0, ((0, 512),)),
        "weight": bell_draw(streams_of[1], (F, F), F ** -0.5, 0.375),
        "tiles": bell_draw(streams_of[2], (N_ROW, N_COL, TPD // 2, TILE, 2 * TILE), (TPD * TILE * TILE // S) ** -0.5, 0.0546875, ((0, 32), (1, 16))),
        "tile_rows": touch_ends(jax.random.randint(streams_of[3], (N_ROW, N_COL, TPD), 0, ROWT), jax.random.fold_in(streams_of[3], 1), 0, ROWT - 1).astype(jnp.int32),
        "tile_cols": touch_ends(jax.random.randint(streams_of[4], (N_ROW, N_COL, TPD), 0, COLT), jax.random.fold_in(streams_of[4], 1), 0, COLT - 1).astype(jnp.int32),
        "counts": draw_counts(jax.random.fold_in(streams_of[6], 71), 0),
    }


def reference(features, weight, tiles, tile_rows, tile_cols, counts):
    product = jnp.dot(features, weight, preferred_element_type=jnp.float32).astype(jnp.bfloat16)
    blocked = product.reshape(N_ROW, N_COL, S, F)
    row_tiles = N_COL * S // TILE
    col_tiles = N_ROW * S // TILE
    slot_index = jnp.arange(TPD, dtype=jnp.int32)

    def grid_row(carry, row_index):
        def add_column(total, col_index):
            column = lax.dynamic_index_in_dim(blocked, col_index, axis=1, keepdims=False)
            column = column.reshape(col_tiles, TILE, F)
            tile_pairs = tiles[row_index, col_index].astype(jnp.float32).reshape(TPD // 2, TILE, 2, TILE)
            picked = column[tile_cols[row_index, col_index]].astype(jnp.float32).reshape(TPD // 2, 2, TILE, F)
            terms = jnp.einsum('qajb,qjbf->qjaf', tile_pairs, picked).reshape(TPD, TILE, F)
            in_use = (slot_index < counts[row_index, col_index]).astype(jnp.float32)
            terms = terms * in_use[:, None, None]
            total = total + jax.ops.segment_sum(terms, tile_rows[row_index, col_index], num_segments=row_tiles)
            return total, None

        start = jnp.zeros((row_tiles, TILE, F), jnp.float32)
        total, unused = lax.scan(add_column, start, jnp.arange(N_COL, dtype=jnp.int32))
        result = jnp.maximum(total, 0.0).astype(jnp.bfloat16).reshape(row_tiles * TILE, F)
        return carry, result

    carry, rows_out = lax.scan(grid_row, jnp.zeros((), jnp.float32), jnp.arange(N_ROW, dtype=jnp.int32))
    return rows_out.reshape(N_ROW * N_COL * S, F)
```

```python
import jax
import jax.numpy as jnp
from jax import lax
from jax.experimental import pallas as pl
from jax.experimental.pallas import tpu as pltpu
from jax.sharding import PartitionSpec as P

TILE = 64
Y_CHIPS, X_CHIPS, CORES = 4, 4, 2
UNROLL = 4
CHUNKS = 8


def row_shift(dy, dx, dcore):
    pairs = []
    for source in range(Y_CHIPS * X_CHIPS * CORES):
        y, x, core = source // (X_CHIPS * CORES), source // CORES % X_CHIPS, source % CORES
        y, x, core = (y + dy) % Y_CHIPS, (x + dx) % X_CHIPS, (core + dcore) % CORES
        pairs.append((source, (y * X_CHIPS + x) * CORES + core))
    return pairs


def shift(value, dy, dx, dcore):
    return lax.ppermute(value, "row", row_shift(dy, dx, dcore))


def spmm_kernel(rows, cols, live, *refs):
    parts, tiles_hbm, out, table, tiles, total, part_sem, tile_sem = refs[:8], *refs[8:]
    part_tiles = table.shape[0] // len(parts)
    pair_chunk = tiles.shape[0] // CHUNKS
    part_copies = [
        pltpu.make_async_copy(part, table.at[pl.ds(i * part_tiles, part_tiles)], part_sem.at[i])
        for i, part in enumerate(parts)
    ]
    tile_copies = [
        pltpu.make_async_copy(
            tiles_hbm.at[pl.ds(i * pair_chunk, pair_chunk)],
            tiles.at[pl.ds(i * pair_chunk, pair_chunk)],
            tile_sem.at[i],
        )
        for i in range(CHUNKS)
    ]
    for copy in part_copies + tile_copies:
        copy.start()
    total[...] = jnp.zeros_like(total)
    lane = lax.broadcasted_iota(jnp.int32, (TILE, 2 * TILE), 1)
    low = (lane < TILE).astype(jnp.bfloat16)
    high = (lane >= TILE).astype(jnp.bfloat16)
    for copy in part_copies:
        copy.wait()
    steps = (live[0] + 2 * UNROLL - 1) // (2 * UNROLL)
    chunk_steps = pair_chunk // UNROLL

    for chunk in range(CHUNKS):
        tile_copies[chunk].wait()

        def step(i, carry):
            first = (chunk * chunk_steps + i) * UNROLL
            terms = []
            for j in range(UNROLL):
                pair = first + j
                block = tiles[pair]
                left = jnp.concatenate([block * low, block * high], axis=0)
                right = jnp.concatenate([table[cols[2 * pair]], table[cols[2 * pair + 1]]], axis=0)
                terms.append(jnp.dot(left, right, preferred_element_type=jnp.float32))
            for j in range(UNROLL):
                pair = first + j
                total[rows[2 * pair]] += terms[j][:TILE]
                total[rows[2 * pair + 1]] += terms[j][TILE:]
            return carry

        lax.fori_loop(0, jnp.clip(steps - chunk * chunk_steps, 0, chunk_steps), step, 0)
    row_tiles = out.shape[0] // TILE
    out[...] = total[:row_tiles].reshape(out.shape).astype(out.dtype)


def body(features, weight, tiles, tile_rows, tile_cols, counts):
    own, width = features.shape
    slots = tile_rows.shape[2]
    n_col = lax.axis_size("col")
    row_tiles = n_col * own // TILE
    own_tiles = own // TILE
    me = lax.axis_index("row")
    my_y, my_x, my_core = me // (X_CHIPS * CORES), me // CORES % X_CHIPS, me % CORES

    product = jnp.dot(features, weight, preferred_element_type=jnp.float32).astype(jnp.bfloat16)
    column = jnp.concatenate([product] + [shift(product, k, 0, 0) for k in (1, 2, 3)], axis=0)
    near = [column, shift(column, 0, 1, 0), shift(column, 0, 3, 0), shift(column, 0, 2, 0)]
    far = [shift(v, 0, 0, 1) for v in near]
    parts = [v.reshape(-1, TILE, width) for v in near + far]

    live = counts[0]
    rows = jnp.where(jnp.arange(slots, dtype=jnp.int32) < live, tile_rows[0, 0], row_tiles)
    block, inner = tile_cols[0, 0] // own_tiles, tile_cols[0, 0] % own_tiles
    y, x, core = block // (X_CHIPS * CORES), block // CORES % X_CHIPS, block % CORES
    back_y, back_x = (my_y - y) % Y_CHIPS, (my_x - x) % X_CHIPS
    place_x = jnp.where(back_x >= 2, 5 - back_x, back_x)
    cols = (((core + my_core) % 2 * X_CHIPS + place_x) * Y_CHIPS + back_y) * own_tiles + inner

    scalar = pl.BlockSpec(memory_space=pltpu.SMEM)
    hbm = pl.BlockSpec(memory_space=pl.ANY)
    partial_rows = pl.pallas_call(
        spmm_kernel,
        out_shape=jax.ShapeDtypeStruct((row_tiles * TILE, width), jnp.bfloat16),
        in_specs=[scalar] * 3 + [hbm] * 9,
        out_specs=pl.BlockSpec(memory_space=pltpu.VMEM),
        scratch_shapes=[
            pltpu.VMEM((8 * parts[0].shape[0], TILE, width), jnp.bfloat16),
            pltpu.VMEM(tiles.shape[2:], jnp.bfloat16),
            pltpu.VMEM((row_tiles + 1, TILE, width), jnp.float32),
            pltpu.SemaphoreType.DMA((8,)),
            pltpu.SemaphoreType.DMA((CHUNKS,)),
        ],
        compiler_params=pltpu.CompilerParams(vmem_limit_bytes=32 << 20),
    )(rows, cols, live, *parts, tiles[0, 0])

    received = lax.all_to_all(partial_rows, "col", 0, 0, tiled=True)
    received = received.reshape(n_col, own, width).astype(jnp.float32)
    return jnp.maximum(jnp.sum(received, axis=0), 0.0).astype(jnp.bfloat16)


def solution(mesh):
    return jax.shard_map(
        body,
        mesh=mesh,
        in_specs=(
            P(("row", "col"), None),
            P(),
            P("row", "col", None, None, None),
            P("row", "col", None),
            P("row", "col", None),
            P("row", "col"),
        ),
        out_specs=P(("row", "col"), None),
        check_vma=False,
    )
```

```python
import functools

import jax
import jax.numpy as jnp
from jax import lax
from jax.experimental import pallas as pl
from jax.experimental.pallas import tpu as pltpu
from jax.sharding import PartitionSpec as P

TILE = 64
Y_CHIPS, X_CHIPS, CORES = 4, 4, 2
UNROLL = 4
CHUNKS = 8


def row_shift(dy, dx, dcore):
    pairs = []
    for source in range(Y_CHIPS * X_CHIPS * CORES):
        y, x, core = source // (X_CHIPS * CORES), source // CORES % X_CHIPS, source % CORES
        y, x, core = (y + dy) % Y_CHIPS, (x + dx) % X_CHIPS, (core + dcore) % CORES
        pairs.append((source, (y * X_CHIPS + x) * CORES + core))
    return pairs


def shift(value, dy, dx, dcore):
    return lax.ppermute(value, "row", row_shift(dy, dx, dcore))


def z_groups(n_col):
    return [[z * 2 + half for z in range(n_col // 2)] for half in range(2)]


def spmm_kernel(lane_block, rows, cols, live, half, *refs):
    n_parts = 8
    parts, tiles_hbm = refs[:n_parts], refs[n_parts]
    outs, (table, tiles, total, part_sem, tile_sem) = refs[n_parts + 1 : -5], refs[-5:]
    part_tiles = table.shape[0] // n_parts
    width = table.shape[2]
    pair_chunk = tiles.shape[0] // CHUNKS
    part_copies = [
        pltpu.make_async_copy(
            part.at[:, :, pl.ds(lane_block * width, width)],
            table.at[pl.ds(i * part_tiles, part_tiles)],
            part_sem.at[i],
        )
        for i, part in enumerate(parts)
    ]
    tile_copies = [
        pltpu.make_async_copy(
            tiles_hbm.at[pl.ds(i * pair_chunk, pair_chunk)],
            tiles.at[pl.ds(i * pair_chunk, pair_chunk)],
            tile_sem.at[i],
        )
        for i in range(CHUNKS)
    ]
    for copy in part_copies + tile_copies:
        copy.start()
    total[...] = jnp.zeros_like(total)
    lane = lax.broadcasted_iota(jnp.int32, (TILE, 2 * TILE), 1)
    low = (lane < TILE).astype(jnp.bfloat16)
    high = (lane >= TILE).astype(jnp.bfloat16)
    for copy in part_copies:
        copy.wait()
    steps = (live[0] + 2 * UNROLL - 1) // (2 * UNROLL)
    chunk_steps = pair_chunk // UNROLL

    for chunk in range(CHUNKS):
        tile_copies[chunk].wait()

        def step(i, carry):
            first = (chunk * chunk_steps + i) * UNROLL
            terms = []
            for j in range(UNROLL):
                pair = first + j
                block = tiles[pair]
                left = jnp.concatenate([block * low, block * high], axis=0)
                right = jnp.concatenate([table[cols[2 * pair]], table[cols[2 * pair + 1]]], axis=0)
                terms.append(jnp.dot(left, right, preferred_element_type=jnp.float32))
            for j in range(UNROLL):
                pair = first + j
                total[rows[2 * pair]] += terms[j][:TILE]
                total[rows[2 * pair + 1]] += terms[j][TILE:]
            return carry

        lax.fori_loop(0, jnp.clip(steps - chunk * chunk_steps, 0, chunk_steps), step, 0)

    row_tiles = total.shape[0] - 1
    if len(outs) == 1:
        outs[0][...] = total[:row_tiles].astype(outs[0].dtype)
    else:
        n_blocks = outs[0].shape[0]
        block_tiles = outs[0].shape[1]
        for z in range(n_blocks):
            for out, side in zip(outs, (half[0], 1 - half[0])):
                first = (2 * z + side) * block_tiles
                out[z] = total[pl.ds(first, block_tiles)].astype(out.dtype)


def spmm(lane_block, rows, cols, live, half, parts, tiles, row_tiles, outs):
    width = parts[0].shape[2] // 2
    scalar = pl.BlockSpec(memory_space=pltpu.SMEM)
    anywhere = pl.BlockSpec(memory_space=pl.ANY)
    flops = 2 * 2 * tiles.size * width
    return pl.pallas_call(
        functools.partial(spmm_kernel, lane_block),
        out_shape=outs,
        in_specs=[scalar] * 4 + [anywhere] * len(parts) + [pl.BlockSpec(memory_space=pltpu.HBM)],
        out_specs=[pl.BlockSpec(memory_space=pltpu.VMEM)] * len(outs),
        scratch_shapes=[
            pltpu.VMEM((len(parts) * parts[0].shape[0], TILE, width), jnp.bfloat16),
            pltpu.VMEM(tiles.shape, jnp.bfloat16),
            pltpu.VMEM((row_tiles + 1, TILE, width), jnp.float32),
            pltpu.SemaphoreType.DMA((len(parts),)),
            pltpu.SemaphoreType.DMA((CHUNKS,)),
        ],
        compiler_params=pltpu.CompilerParams(vmem_limit_bytes=36 << 20),
        cost_estimate=pl.CostEstimate(flops=flops, bytes_accessed=8 << 20, transcendentals=0),
    )(rows, cols, live, half, *parts, tiles)


def body(features, weight, tiles, tile_rows, tile_cols, counts):
    own, width = features.shape
    slots = tile_rows.shape[2]
    n_col = lax.axis_size("col")
    n_z = n_col // 2
    row_tiles = n_col * own // TILE
    own_tiles = own // TILE
    lanes = width // 2
    me = lax.axis_index("row")
    my_y, my_x, my_core = me // (X_CHIPS * CORES), me // CORES % X_CHIPS, me % CORES
    my_half = lax.axis_index("col") % 2
    other_half = [(c, c ^ 1) for c in range(n_col)]

    product = jnp.dot(features, weight, preferred_element_type=jnp.float32).astype(jnp.bfloat16)
    pieces = [product] + [shift(product, k, 0, 0) for k in (1, 2, 3)]

    live = counts[0]
    rows = jnp.where(jnp.arange(slots, dtype=jnp.int32) < live, tile_rows[0, 0], row_tiles)
    block, inner = tile_cols[0, 0] // own_tiles, tile_cols[0, 0] % own_tiles
    y, x, core = block // (X_CHIPS * CORES), block // CORES % X_CHIPS, block % CORES
    back_y, back_x = (my_y - y) % Y_CHIPS, (my_x - x) % X_CHIPS
    place_x = jnp.where(back_x >= 2, 5 - back_x, back_x)
    cols = (((core + my_core) % 2 * X_CHIPS + place_x) * Y_CHIPS + back_y) * own_tiles + inner
    *pieces, rows, cols = lax.optimization_barrier((*pieces, rows, cols))

    column = jnp.concatenate(pieces, axis=0)
    near = [column, shift(column, 0, 1, 0), shift(column, 0, 3, 0), shift(column, 0, 2, 0)]
    far = [shift(v, 0, 0, 1) for v in near]
    parts = [v.reshape(-1, TILE, width) for v in near + far]

    def call(lane_block, outs):
        half = my_half.reshape(1).astype(jnp.int32)
        return spmm(lane_block, rows, cols, live, half, parts, tiles[0, 0], row_tiles, outs)

    kept = jax.ShapeDtypeStruct((n_z, own_tiles, TILE, lanes), jnp.float32)
    sent = jax.ShapeDtypeStruct((n_z, own_tiles, TILE, lanes), jnp.bfloat16)
    near_sum, far_sum = call(0, [kept, sent])
    arrived = lax.ppermute(far_sum, "col", other_half)

    whole = jax.ShapeDtypeStruct((row_tiles, TILE, lanes), jnp.bfloat16)
    (second,) = call(1, [whole])
    groups = z_groups(n_col)
    second = lax.all_to_all(
        second.reshape(n_z, 2, own, lanes), "col", 0, 0, axis_index_groups=groups, tiled=True
    )
    second = jnp.sum(second.astype(jnp.float32), axis=0)
    keep = jnp.where(my_half == 0, second[0], second[1])
    send = jnp.where(my_half == 0, second[1], second[0]).astype(jnp.bfloat16)
    second = keep + lax.ppermute(send, "col", other_half).astype(jnp.float32)

    first = (near_sum + arrived.astype(jnp.float32)).astype(jnp.bfloat16)
    first = lax.all_to_all(
        first.reshape(n_z, own, lanes), "col", 0, 0, axis_index_groups=groups, tiled=True
    )
    first = jnp.sum(first.astype(jnp.float32), axis=0)
    return jnp.maximum(jnp.concatenate([first, second], axis=1), 0.0).astype(jnp.bfloat16)


def solution(mesh):
    return jax.shard_map(
        body,
        mesh=mesh,
        in_specs=(
            P(("row", "col"), None),
            P(),
            P("row", "col", None, None, None),
            P("row", "col", None),
            P("row", "col", None),
            P("row", "col"),
        ),
        out_specs=P(("row", "col"), None),
        check_vma=False,
    )
```

```python
import jax
import jax.numpy as jnp
from jax import lax
from jax.experimental import pallas as pl
from jax.experimental.pallas import tpu as pltpu
from jax.sharding import PartitionSpec as P

TILE = 64
Y_CHIPS, X_CHIPS, CORES = 4, 4, 2
GROUP = 4
UNROLL = 8
CHUNKS = 4


def shift(value, dy, dx):
    pairs = []
    for source in range(Y_CHIPS * X_CHIPS * CORES):
        y, x, core = source // (X_CHIPS * CORES), source // CORES % X_CHIPS, source % CORES
        y, x = (y + dy) % Y_CHIPS, (x + dx) % X_CHIPS
        pairs.append((source, (y * X_CHIPS + x) * CORES + core))
    return lax.ppermute(value, "row", pairs)


def both_cores(value):
    groups = [[2 * chip, 2 * chip + 1] for chip in range(Y_CHIPS * X_CHIPS)]
    return lax.all_gather(value, "row", axis_index_groups=groups, axis=0, tiled=True)


def count(mask, axis):
    return jnp.sum(mask.astype(jnp.int32), axis=axis)


def plan(rows, cols, live, row_tiles):
    slots = rows.shape[0]
    groups = (slots + row_tiles) // 2
    groups = (groups + UNROLL - 1) // UNROLL * UNROLL
    slot = jnp.arange(slots, dtype=jnp.int32)
    odd = slot % 2
    row = jnp.where(slot < live, rows, row_tiles)
    key = row * 2 + odd
    rank = count((key[None, :] == key[:, None]) & (slot[None, :] < slot[:, None]), 1)
    row_id = jnp.arange(row_tiles, dtype=jnp.int32)
    evens = count(key[None, :] == 2 * row_id[:, None], 1)
    odds = count(key[None, :] == 2 * row_id[:, None] + 1, 1)
    held = (jnp.maximum(evens, odds) + 1) // 2
    ends = jnp.sum(jnp.where(row_id[None, :] <= row_id[:, None], held[None, :], 0), axis=1)
    base = jnp.sum(jnp.where(row_id[None, :] < row[:, None], held[None, :], 0), axis=1)
    place = jnp.where(slot < live, base * GROUP + rank * 2 + odd, groups * GROUP)
    spot = jnp.arange(groups * GROUP, dtype=jnp.int32)
    found = jnp.where(place[None, :] == spot[:, None], slot[None, :] * 128 + cols[None, :], -1)
    found = jnp.max(found, axis=1)
    block = jnp.where(found < 0, slots // 2, found // 256)
    column = jnp.where(found < 0, 0, found % 128)
    group = jnp.arange(groups, dtype=jnp.int32)
    group_row = count(ends[None, :] <= group[:, None], 1)
    return block, column, group_row, ends[row_tiles - 1 :]


def spmm_kernel(block, column, group_row, used, *refs):
    parts, tiles_hbm, out, table, tiles, total, sems = refs[:-6], *refs[-6:]
    pairs = tiles_hbm.shape[0]
    chunk = pairs // CHUNKS
    copies = [
        pltpu.make_async_copy(
            tiles_hbm.at[pl.ds(i * chunk, chunk)], tiles.at[pl.ds(i * chunk, chunk)], sems.at[i]
        )
        for i in range(CHUNKS)
    ]
    for copy in copies:
        copy.start()
    tiles[pairs] = jnp.zeros(tiles.shape[1:], tiles.dtype)
    total[...] = jnp.zeros_like(total)
    part_tiles = table.shape[0] // len(parts)
    for i, part in enumerate(parts):
        table[pl.ds(i * part_tiles, part_tiles)] = part[...]
    left = lax.broadcasted_iota(jnp.int32, (TILE, 2 * TILE), 1) < TILE
    for copy in copies:
        copy.wait()

    def step(i, carry):
        terms = []
        for j in range(UNROLL):
            spots = [(i * UNROLL + j) * GROUP + t for t in range(GROUP)]
            lhs = [
                jnp.where(left, tiles[block[spots[t]]], tiles[block[spots[t + 1]]])
                for t in range(0, GROUP, 2)
            ]
            rhs = [table[column[spot]] for spot in spots]
            terms.append(
                jnp.dot(
                    jnp.concatenate(lhs, axis=1),
                    jnp.concatenate(rhs, axis=0),
                    preferred_element_type=jnp.float32,
                )
            )
        for j in range(UNROLL):
            total[group_row[i * UNROLL + j]] += terms[j]
        return carry

    lax.fori_loop(0, (used[0] + UNROLL - 1) // UNROLL, step, 0)
    row_tiles = out.shape[0] // TILE
    out[...] = total[:row_tiles].reshape(out.shape).astype(out.dtype)


def spmm(block, column, group_row, used, parts, tiles, row_tiles):
    width = parts[0].shape[2]
    scalar = pl.BlockSpec(memory_space=pltpu.SMEM)
    vmem = pl.BlockSpec(memory_space=pltpu.VMEM)
    return pl.pallas_call(
        spmm_kernel,
        out_shape=jax.ShapeDtypeStruct((row_tiles * TILE, width), jnp.bfloat16),
        in_specs=[scalar] * 4 + [vmem] * len(parts) + [pl.BlockSpec(memory_space=pl.ANY)],
        out_specs=vmem,
        scratch_shapes=[
            pltpu.VMEM((len(parts) * parts[0].shape[0], TILE, width), jnp.bfloat16),
            pltpu.VMEM((tiles.shape[0] + 1, *tiles.shape[1:]), jnp.bfloat16),
            pltpu.VMEM((row_tiles + 1, TILE, width), jnp.float32),
            pltpu.SemaphoreType.DMA((CHUNKS,)),
        ],
        compiler_params=pltpu.CompilerParams(vmem_limit_bytes=VMEM_LIMIT),
    )(block, column, group_row, used, *parts, tiles)


VMEM_LIMIT = 48 << 20


def body(features, weight, tiles, tile_rows, tile_cols, counts):
    own, width = features.shape
    n_col = lax.axis_size("col")
    row_tiles = n_col * own // TILE
    own_tiles = own // TILE
    me = lax.axis_index("row")
    my_y, my_x = me // (X_CHIPS * CORES), me // CORES % X_CHIPS

    product = jnp.dot(features, weight, preferred_element_type=jnp.float32).astype(jnp.bfloat16)
    pieces = [product] + [shift(product, k, 0) for k in (1, 2, 3)]

    owner, inner = tile_cols[0, 0] // own_tiles, tile_cols[0, 0] % own_tiles
    y, x, core = owner // (X_CHIPS * CORES), owner // CORES % X_CHIPS, owner % CORES
    back_y, back_x = (my_y - y) % Y_CHIPS, (my_x - x) % X_CHIPS
    place_x = jnp.where(back_x >= 2, 5 - back_x, back_x)
    cols = ((place_x * CORES + core) * Y_CHIPS + back_y) * own_tiles + inner
    block, column, group_row, used = plan(tile_rows[0, 0], cols, counts[0, 0], row_tiles)
    *pieces, block, column, group_row, used = lax.optimization_barrier(
        (*pieces, block, column, group_row, used)
    )

    line = jnp.concatenate(pieces, axis=0)
    near = [line, shift(line, 0, 1), shift(line, 0, 3), shift(line, 0, 2)]
    parts = [both_cores(v).reshape(-1, TILE, width) for v in near]
    partial_rows = spmm(block, column, group_row, used, parts, tiles[0, 0], row_tiles)

    received = lax.all_to_all(partial_rows, "col", 0, 0, tiled=True)
    received = received.reshape(n_col, own, width).astype(jnp.float32)
    return jnp.maximum(jnp.sum(received, axis=0), 0.0).astype(jnp.bfloat16)


def solution(mesh):
    return jax.shard_map(
        body,
        mesh=mesh,
        in_specs=(
            P(("row", "col"), None),
            P(),
            P("row", "col", None, None, None),
            P("row", "col", None),
            P("row", "col", None),
            P("row", "col"),
        ),
        out_specs=P(("row", "col"), None),
        check_vma=False,
    )
```

```python
import functools

import jax
import jax.numpy as jnp
from jax import lax
from jax.experimental import pallas as pl
from jax.experimental.pallas import tpu as pltpu
from jax.sharding import PartitionSpec as P

TILE = 64
Y_CHIPS, X_CHIPS, CORES = 4, 4, 2
GROUP = 4
UNROLL = 8
CHUNKS = 4


def shift(value, dy, dx):
    pairs = []
    for source in range(Y_CHIPS * X_CHIPS * CORES):
        y, x, core = source // (X_CHIPS * CORES), source // CORES % X_CHIPS, source % CORES
        y, x = (y + dy) % Y_CHIPS, (x + dx) % X_CHIPS
        pairs.append((source, (y * X_CHIPS + x) * CORES + core))
    return lax.ppermute(value, "row", pairs)


def both_cores(value):
    groups = [[2 * chip, 2 * chip + 1] for chip in range(Y_CHIPS * X_CHIPS)]
    return lax.all_gather(value, "row", axis_index_groups=groups, axis=0, tiled=True)


def count(mask, axis):
    return jnp.sum(mask.astype(jnp.int32), axis=axis)


def place_slots(rows, late, live, row_tiles):
    keys = 2 * row_tiles
    slot = jnp.arange(rows.shape[0], dtype=jnp.int32)
    odd = slot % 2
    key = jnp.where(slot < live, late * row_tiles + rows, keys)
    full_key = key * 2 + odd
    rank = count((full_key[None, :] == full_key[:, None]) & (slot[None, :] < slot[:, None]), 1)
    key_id = jnp.arange(keys, dtype=jnp.int32)
    evens = count(full_key[None, :] == 2 * key_id[:, None], 1)
    odds = count(full_key[None, :] == 2 * key_id[:, None] + 1, 1)
    held = (jnp.maximum(evens, odds) + 1) // 2
    early = jnp.sum(jnp.where(key_id < row_tiles, held, 0))
    early_steps = (early + UNROLL - 1) // UNROLL
    gap = early_steps * UNROLL - early
    skip = jnp.where(key_id < row_tiles, 0, gap)
    ends = jnp.sum(jnp.where(key_id[None, :] <= key_id[:, None], held[None, :], 0), axis=1) + skip
    base = jnp.sum(jnp.where(key_id[None, :] < key[:, None], held[None, :], 0), axis=1)
    base = base + jnp.where(key < row_tiles, 0, gap)
    place = jnp.where(slot < live, base * GROUP + rank * 2 + odd, -1)
    return place, ends, jnp.stack([early_steps, (jnp.max(ends) + UNROLL - 1) // UNROLL])


def fill_groups(place, ends, cols, row_tiles):
    slots = place.shape[0]
    groups = (slots + ends.shape[0]) // 2 + UNROLL - 1
    groups = (groups + UNROLL - 1) // UNROLL * UNROLL
    slot = jnp.arange(slots, dtype=jnp.int32)
    spot = jnp.arange(groups * GROUP, dtype=jnp.int32)
    found = jnp.where(place[None, :] == spot[:, None], slot[None, :] * 128 + cols[None, :], -1)
    found = jnp.max(found, axis=1)
    block = jnp.where(found < 0, slots // 2, found // 256)
    column = jnp.where(found < 0, 0, found % 128)
    group = jnp.arange(groups, dtype=jnp.int32)
    group_row = count(ends[None, :] <= group[:, None], 1) % row_tiles
    return block, column, group_row


def tile_copies(tiles_hbm, tiles, sems):
    chunk = tiles_hbm.shape[0] // CHUNKS
    return [
        pltpu.make_async_copy(
            tiles_hbm.at[pl.ds(i * chunk, chunk)], tiles.at[pl.ds(i * chunk, chunk)], sems.at[i]
        )
        for i in range(CHUNKS)
    ]


def fill_table(table, parts, weight):
    part_tiles, _, depth = parts[0].shape
    step = 8
    for i, part in enumerate(parts):

        def some(k, carry):
            rows = part[pl.ds(k * step, step)].reshape(step * TILE, depth)
            made = jnp.dot(rows, weight[...], preferred_element_type=jnp.float32)
            made = made.astype(table.dtype).reshape(step, TILE, table.shape[2])
            table[pl.ds(i * part_tiles + k * step, step)] = made
            return carry

        lax.fori_loop(0, part_tiles // step, some, 0)


def add_groups(first, last, block, column, group_row, tiles, table, total):
    left = lax.broadcasted_iota(jnp.int32, (TILE, 2 * TILE), 1) < TILE

    def step(i, carry):
        terms = []
        for j in range(UNROLL):
            spots = [(i * UNROLL + j) * GROUP + t for t in range(GROUP)]
            lhs = [
                jnp.where(left, tiles[block[spots[t]]], tiles[block[spots[t + 1]]])
                for t in range(0, GROUP, 2)
            ]
            rhs = [table[column[spot]] for spot in spots]
            terms.append(
                jnp.dot(
                    jnp.concatenate(lhs, axis=1),
                    jnp.concatenate(rhs, axis=0),
                    preferred_element_type=jnp.float32,
                )
            )
        for j in range(UNROLL):
            total[group_row[i * UNROLL + j]] += terms[j]
        return carry

    lax.fori_loop(first, last, step, 0)


def spmm_kernel(late, block, column, group_row, steps, weight, *refs):
    n_parts = len(refs) - (7 if late else 5)
    parts, tiles_hbm, refs = refs[:n_parts], refs[n_parts], refs[n_parts + 1 :]
    if late:
        before, out, table, tiles, total, sems = refs
    else:
        total, table, tiles, sems = refs
    copies = tile_copies(tiles_hbm, tiles, sems)
    for copy in copies:
        copy.start()
    tiles[tiles_hbm.shape[0]] = jnp.zeros(tiles.shape[1:], tiles.dtype)
    total[...] = before[...] if late else jnp.zeros_like(total)
    fill_table(table, parts, weight)
    for copy in copies:
        copy.wait()
    first, last = (steps[0], steps[1]) if late else (0, steps[0])
    add_groups(first, last, block, column, group_row, tiles, table, total)
    if late:
        out[...] = total[...].reshape(out.shape).astype(out.dtype)


def spmm(plan, weight, parts, tiles, row_tiles, before=None):
    width = weight.shape[1]
    scalar = pl.BlockSpec(memory_space=pltpu.SMEM)
    vmem = pl.BlockSpec(memory_space=pltpu.VMEM)
    anywhere = pl.BlockSpec(memory_space=pl.ANY)
    sums = (row_tiles, TILE, width)
    scratch = [
        pltpu.VMEM((len(parts) * parts[0].shape[0], TILE, width), jnp.bfloat16),
        pltpu.VMEM((tiles.shape[0] + 1, *tiles.shape[1:]), tiles.dtype),
    ]
    late = before is not None
    if late:
        scratch.append(pltpu.VMEM(sums, jnp.float32))
        out = jax.ShapeDtypeStruct((row_tiles * TILE, width), jnp.bfloat16)
    else:
        out = jax.ShapeDtypeStruct(sums, jnp.float32)
    return pl.pallas_call(
        functools.partial(spmm_kernel, late),
        out_shape=out,
        in_specs=[scalar] * len(plan) + [vmem] * (1 + len(parts)) + [anywhere] + [vmem] * late,
        out_specs=vmem,
        scratch_shapes=scratch + [pltpu.SemaphoreType.DMA((CHUNKS,))],
        compiler_params=pltpu.CompilerParams(vmem_limit_bytes=SPMM_VMEM),
        name="late_groups" if late else "early_groups",
    )(*plan, weight, *parts, tiles, *([before] if late else []))


SPMM_VMEM = 46 << 20


def body(features, weight, tiles, tile_rows, tile_cols, counts):
    own, width = features.shape
    n_col = lax.axis_size("col")
    row_tiles = n_col * own // TILE
    own_tiles = own // TILE
    me = lax.axis_index("row")
    my_y, my_x = me // (X_CHIPS * CORES), me // CORES % X_CHIPS

    def part(value):
        return both_cores(value).reshape(-1, TILE, width)

    owner, inner = tile_cols[0, 0] // own_tiles, tile_cols[0, 0] % own_tiles
    y, x, core = owner // (X_CHIPS * CORES), owner // CORES % X_CHIPS, owner % CORES
    back_y, back_x = (my_y - y) % Y_CHIPS, (my_x - x) % X_CHIPS
    late = back_x % 2
    cols = ((back_x // 2 ^ late) * CORES + core) * Y_CHIPS * own_tiles
    cols = cols + back_y * own_tiles + inner

    pieces = [features] + [shift(features, k, 0) for k in (1, 2, 3)]
    places = (cols, *place_slots(tile_rows[0, 0], late, counts[0, 0], row_tiles))
    *pieces, cols, place, ends, steps = lax.optimization_barrier((*pieces, *places))
    line = jnp.concatenate(pieces, axis=0)
    across = shift(line, 0, 2)

    own_line, line, cols, place, ends = lax.optimization_barrier(
        (part(line), line, cols, place, ends)
    )
    behind, ahead = shift(line, 0, 1), shift(line, 0, 3)
    groups = fill_groups(place, ends, cols, row_tiles)
    across, *groups = lax.optimization_barrier((across, *groups))

    plan = (*groups, steps)
    early = spmm(plan, weight, [own_line, part(across)], tiles[0, 0], row_tiles)
    early, ahead = lax.optimization_barrier((early, ahead))
    late_parts = [part(ahead), part(behind)]
    partial_rows = spmm(plan, weight, late_parts, tiles[0, 0], row_tiles, early)

    received = lax.all_to_all(partial_rows, "col", 0, 0, tiled=True)
    received = received.reshape(n_col, own, width).astype(jnp.float32)
    return jnp.maximum(jnp.sum(received, axis=0), 0.0).astype(jnp.bfloat16)


def solution(mesh):
    return jax.shard_map(
        body,
        mesh=mesh,
        in_specs=(
            P(("row", "col"), None),
            P(),
            P("row", "col", None, None, None),
            P("row", "col", None),
            P("row", "col", None),
            P("row", "col"),
        ),
        out_specs=P(("row", "col"), None),
        check_vma=False,
    )
```

```python
import functools

import jax
import jax.numpy as jnp
from jax import lax
from jax.experimental import pallas as pl
from jax.experimental.pallas import tpu as pltpu
from jax.sharding import PartitionSpec as P

TILE = 64
Y_CHIPS, X_CHIPS, CORES = 4, 4, 2
GROUP = 4
UNROLL = 8
CHUNKS = 4


def shift(value, dy, dx):
    pairs = []
    for source in range(Y_CHIPS * X_CHIPS * CORES):
        y, x, core = source // (X_CHIPS * CORES), source // CORES % X_CHIPS, source % CORES
        y, x = (y + dy) % Y_CHIPS, (x + dx) % X_CHIPS
        pairs.append((source, (y * X_CHIPS + x) * CORES + core))
    return lax.ppermute(value, "row", pairs)


def both_cores(value):
    groups = [[2 * chip, 2 * chip + 1] for chip in range(Y_CHIPS * X_CHIPS)]
    return lax.all_gather(value, "row", axis_index_groups=groups, axis=0, tiled=True)


def plan_kernel(own_tiles, row_tiles, me, live, rows_hbm, cols_hbm, own_hbm, *refs):
    block, column, group_row, steps, own, rows_ref, cols_ref, sems = refs
    copies = [
        pltpu.make_async_copy(source, target, sems.at[i])
        for i, (source, target) in enumerate(
            ((rows_hbm, rows_ref), (cols_hbm, cols_ref), (own_hbm, own))
        )
    ]
    for copy in copies:
        copy.start()
    for copy in copies:
        copy.wait()
    slots = rows_ref.shape[1]
    keys = 2 * row_tiles

    def iota(rows, lanes, axis):
        return lax.broadcasted_iota(jnp.int32, (rows, lanes), axis)

    def ones(mask):
        return jnp.where(mask, 1.0, 0.0)

    slot = iota(1, slots, 1)
    odd = slot & 1
    alive = slot < live[0, 0]
    owner = (cols_ref[...] * (128 // own_tiles + 1)) >> 7
    inner = cols_ref[...] - owner * own_tiles
    y, x, core = owner // (X_CHIPS * CORES), owner // CORES % X_CHIPS, owner % CORES
    back_y, back_x = (me[0] - y) % Y_CHIPS, (me[1] - x) % X_CHIPS
    late = back_x % 2
    col = ((back_x // 2 ^ late) * CORES + core) * Y_CHIPS * own_tiles + back_y * own_tiles + inner
    key = jnp.where(alive, late * row_tiles + rows_ref[...], keys)

    match = key == iota(keys, slots, 0)
    is_odd = jnp.broadcast_to(odd, (keys, slots)) == 1
    odds = ones(match & is_odd)
    evens = ones(match) - odds
    most = jnp.maximum(jnp.sum(evens, axis=1, keepdims=True), jnp.sum(odds, axis=1, keepdims=True))
    held = (most.astype(jnp.int32) + 1) >> 1
    held = jnp.broadcast_to(held, (keys, 128)).astype(jnp.float32)
    upto = ones(iota(keys, keys, 1) <= iota(keys, keys, 0)).astype(jnp.bfloat16)
    ends = jnp.dot(upto, held.astype(jnp.bfloat16), preferred_element_type=jnp.float32)
    early = ends[row_tiles - 1 : row_tiles].astype(jnp.int32)
    early_steps = (early + UNROLL - 1) >> UNROLL.bit_length() - 1
    gap = (early_steps * UNROLL - early).astype(jnp.float32)
    ends = ends + jnp.where(iota(keys, 128, 0) < row_tiles, 0.0, gap)
    base = ends - held
    last_steps = (ends[keys - 1 :].astype(jnp.int32) + UNROLL - 1) >> UNROLL.bit_length() - 1
    steps[...] = jnp.where(iota(1, 128, 1) == 0, early_steps, last_steps)

    before = ones(iota(slots, slots, 0) < iota(slots, slots, 1)).astype(jnp.bfloat16)
    even_rank = jnp.dot(evens.astype(jnp.bfloat16), before, preferred_element_type=jnp.float32)
    odd_rank = jnp.dot(odds.astype(jnp.bfloat16), before, preferred_element_type=jnp.float32)
    spots = (evens + odds) * base[:, :1] * GROUP + (evens * even_rank + odds * odd_rank) * 2
    place = jnp.sum(spots, axis=0, keepdims=True).astype(jnp.int32) + odd
    place = jnp.where(alive, place, -1)

    n_spots = block.shape[1]
    taken = ones(place == iota(n_spots, slots, 0)).astype(jnp.bfloat16)
    line = iota(8, slots, 0)
    values = jnp.where(line == 0, slot // 2, jnp.where(line == 1, col, jnp.where(line == 2, 1, 0)))
    values = values.astype(jnp.float32).astype(jnp.bfloat16)
    found = lax.dot_general(
        values, taken, (((1,), (1,)), ((), ())), preferred_element_type=jnp.float32
    )
    block[...] = jnp.where(found[2:3] > 0.5, found[:1], float(slots // 2)).astype(jnp.int32)
    column[...] = found[1:2].astype(jnp.int32)
    n_groups = group_row.shape[1]
    passed = ones(ends[:, :1] <= iota(keys, n_groups, 1).astype(jnp.float32))
    row = jnp.sum(passed, axis=0, keepdims=True).astype(jnp.int32)
    row = jnp.where(row < row_tiles, row, row - row_tiles)
    group_row[...] = jnp.where(row < row_tiles, row, 0)


def plan(rows, cols, live, me, own, row_tiles):
    groups = (rows.shape[1] + 2 * row_tiles) // 2 + UNROLL - 1
    spots = (groups * GROUP + 127) // 128 * 128
    scalar = pl.BlockSpec(memory_space=pltpu.SMEM)
    vmem = pl.BlockSpec(memory_space=pltpu.VMEM)
    return pl.pallas_call(
        functools.partial(plan_kernel, own.shape[0] // TILE, row_tiles),
        out_shape=[jax.ShapeDtypeStruct((1, n), jnp.int32) for n in (spots, spots, 384, 128)]
        + [jax.ShapeDtypeStruct(own.shape, own.dtype)],
        in_specs=[scalar] * 2 + [pl.BlockSpec(memory_space=pl.ANY)] * 3,
        out_specs=[vmem] * 5,
        scratch_shapes=[pltpu.VMEM(rows.shape, jnp.int32)] * 2 + [pltpu.SemaphoreType.DMA((3,))],
        compiler_params=pltpu.CompilerParams(vmem_limit_bytes=40 << 20),
        name="plan",
    )(me, live, rows, cols, own)


def tile_copies(tiles_hbm, tiles, sems):
    chunk = tiles_hbm.shape[0] // CHUNKS
    return [
        pltpu.make_async_copy(
            tiles_hbm.at[pl.ds(i * chunk, chunk)], tiles.at[pl.ds(i * chunk, chunk)], sems.at[i]
        )
        for i in range(CHUNKS)
    ]


def fill_table(table, parts, weight):
    part_tiles, _, depth = parts[0].shape
    step = 8
    for i, part in enumerate(parts):

        def some(k, carry):
            rows = part[pl.ds(k * step, step)].reshape(step * TILE, depth)
            made = jnp.dot(rows, weight[...], preferred_element_type=jnp.float32)
            made = made.astype(table.dtype).reshape(step, TILE, table.shape[2])
            table[pl.ds(i * part_tiles + k * step, step)] = made
            return carry

        lax.fori_loop(0, part_tiles // step, some, 0)


def add_groups(first, last, block, column, group_row, tiles, table, total):
    left = lax.broadcasted_iota(jnp.int32, (TILE, 2 * TILE), 1) < TILE

    def step(i, carry):
        terms = []
        for j in range(UNROLL):
            spots = [(i * UNROLL + j) * GROUP + t for t in range(GROUP)]
            lhs = [
                jnp.where(left, tiles[block[0, spots[t]]], tiles[block[0, spots[t + 1]]])
                for t in range(0, GROUP, 2)
            ]
            rhs = [table[column[0, spot]] for spot in spots]
            terms.append(
                jnp.dot(
                    jnp.concatenate(lhs, axis=1),
                    jnp.concatenate(rhs, axis=0),
                    preferred_element_type=jnp.float32,
                )
            )
        for j in range(UNROLL):
            total[group_row[0, i * UNROLL + j]] += terms[j]
        return carry

    lax.fori_loop(first, last, step, 0)


def spmm_kernel(late, block, column, group_row, steps, weight, *refs):
    n_parts = len(refs) - (7 if late else 5)
    parts, tiles_hbm, refs = refs[:n_parts], refs[n_parts], refs[n_parts + 1 :]
    if late:
        before, out, table, tiles, total, sems = refs
    else:
        total, table, tiles, sems = refs
    copies = tile_copies(tiles_hbm, tiles, sems)
    for copy in copies:
        copy.start()
    tiles[tiles_hbm.shape[0]] = jnp.zeros(tiles.shape[1:], tiles.dtype)
    total[...] = before[...] if late else jnp.zeros_like(total)
    fill_table(table, parts, weight)
    for copy in copies:
        copy.wait()
    first, last = (steps[0, 0], steps[0, 1]) if late else (0, steps[0, 0])
    add_groups(first, last, block, column, group_row, tiles, table, total)
    if late:
        out[...] = total[...].reshape(out.shape).astype(out.dtype)


def spmm(plan, weight, parts, tiles, row_tiles, before=None):
    width = weight.shape[1]
    scalar = pl.BlockSpec(memory_space=pltpu.SMEM)
    vmem = pl.BlockSpec(memory_space=pltpu.VMEM)
    anywhere = pl.BlockSpec(memory_space=pl.ANY)
    sums = (row_tiles, TILE, width)
    scratch = [
        pltpu.VMEM((len(parts) * parts[0].shape[0], TILE, width), jnp.bfloat16),
        pltpu.VMEM((tiles.shape[0] + 1, *tiles.shape[1:]), tiles.dtype),
    ]
    late = before is not None
    if late:
        scratch.append(pltpu.VMEM(sums, jnp.float32))
        out = jax.ShapeDtypeStruct((row_tiles * TILE, width), jnp.bfloat16)
    else:
        out = jax.ShapeDtypeStruct(sums, jnp.float32)
    return pl.pallas_call(
        functools.partial(spmm_kernel, late),
        out_shape=out,
        in_specs=[scalar] * len(plan) + [vmem] * (1 + len(parts)) + [anywhere] + [vmem] * late,
        out_specs=vmem,
        scratch_shapes=scratch + [pltpu.SemaphoreType.DMA((CHUNKS,))],
        compiler_params=pltpu.CompilerParams(vmem_limit_bytes=SPMM_VMEM),
        name="late_groups" if late else "early_groups",
    )(*plan, weight, *parts, tiles, *([before] if late else []))


SPMM_VMEM = 46 << 20


def body(features, weight, tiles, tile_rows, tile_cols, counts):
    own, width = features.shape
    n_col = lax.axis_size("col")
    row_tiles = n_col * own // TILE
    me = lax.axis_index("row")
    my_y, my_x = me // (X_CHIPS * CORES), me // CORES % X_CHIPS

    def part(value):
        return both_cores(value).reshape(-1, TILE, width)

    pieces = [shift(features, k, 0) for k in (1, 2, 3)]
    place = jnp.stack([my_y, my_x]).astype(jnp.int32)
    *groups, own_rows = plan(tile_rows[0], tile_cols[0], counts, place, features, row_tiles)
    *pieces, block, column, group_row, steps = lax.optimization_barrier(
        (own_rows, *pieces, *groups)
    )
    line = jnp.concatenate(pieces, axis=0)
    across = shift(line, 0, 2)
    own_line, line = lax.optimization_barrier((part(line), line))
    behind, ahead = shift(line, 0, 1), shift(line, 0, 3)

    groups = (block, column, group_row, steps)
    early = spmm(groups, weight, [own_line, part(across)], tiles[0, 0], row_tiles)
    early, ahead = lax.optimization_barrier((early, ahead))
    late_parts = [part(ahead), part(behind)]
    partial_rows = spmm(groups, weight, late_parts, tiles[0, 0], row_tiles, early)

    received = lax.all_to_all(partial_rows, "col", 0, 0, tiled=True)
    received = received.reshape(n_col, own, width).astype(jnp.float32)
    return jnp.maximum(jnp.sum(received, axis=0), 0.0).astype(jnp.bfloat16)


def solution(mesh):
    return jax.shard_map(
        body,
        mesh=mesh,
        in_specs=(
            P(("row", "col"), None),
            P(),
            P("row", "col", None, None, None),
            P("row", "col", None),
            P("row", "col", None),
            P("row", "col"),
        ),
        out_specs=P(("row", "col"), None),
        check_vma=False,
    )
```

```python
import functools

import jax
import jax.numpy as jnp
from jax import lax
from jax.experimental import pallas as pl
from jax.experimental.pallas import tpu as pltpu
from jax.sharding import PartitionSpec as P

TILE = 64
Y_CHIPS, X_CHIPS, CORES = 4, 4, 2
HALVES = 2
GROUP = 4
UNROLL = 16
CHUNKS = 4


def shift(value, dy, dx):
    pairs = []
    for source in range(Y_CHIPS * X_CHIPS * CORES):
        y, x, core = source // (X_CHIPS * CORES), source // CORES % X_CHIPS, source % CORES
        y, x = (y + dy) % Y_CHIPS, (x + dx) % X_CHIPS
        pairs.append((source, (y * X_CHIPS + x) * CORES + core))
    return lax.ppermute(value, "row", pairs)


def z_neighbours(n_col, offset):
    n_z = n_col // HALVES
    pairs = []
    for source in range(n_col):
        z, half = source // HALVES, source % HALVES
        z = (z + 1 if z % 2 == offset else z - 1) % n_z
        pairs.append((source, z * HALVES + half))
    return pairs


def both_cores(value):
    groups = [[2 * chip, 2 * chip + 1] for chip in range(Y_CHIPS * X_CHIPS)]
    return lax.all_gather(value, "row", axis_index_groups=groups, axis=0, tiled=True)


def plan_kernel(own_tiles, row_tiles, me, live, rows_hbm, cols_hbm, own_hbm, *refs):
    block, column, group_row, steps, own, rows_ref, cols_ref, sems = refs
    copies = [
        pltpu.make_async_copy(source, target, sems.at[i])
        for i, (source, target) in enumerate(
            ((rows_hbm, rows_ref), (cols_hbm, cols_ref), (own_hbm, own))
        )
    ]
    for copy in copies:
        copy.start()
    for copy in copies:
        copy.wait()
    slots = rows_ref.shape[1]
    keys = 2 * row_tiles

    def iota(rows, lanes, axis):
        return lax.broadcasted_iota(jnp.int32, (rows, lanes), axis)

    def ones(mask):
        return jnp.where(mask, 1.0, 0.0)

    slot = iota(1, slots, 1)
    odd = slot & 1
    alive = slot < live[0, 0]
    owner = (cols_ref[...] * (128 // own_tiles + 1)) >> 7
    inner = cols_ref[...] - owner * own_tiles
    y, x, core = owner // (X_CHIPS * CORES), owner // CORES % X_CHIPS, owner % CORES
    back_y, back_x = (me[0] - y) % Y_CHIPS, (me[1] - x) % X_CHIPS
    late = back_x % 2
    col = ((back_x // 2 ^ late) * CORES + core) * Y_CHIPS * own_tiles + back_y * own_tiles + inner
    key = jnp.where(alive, late * row_tiles + rows_ref[...], keys)

    match = key == iota(keys, slots, 0)
    is_odd = jnp.broadcast_to(odd, (keys, slots)) == 1
    odds = ones(match & is_odd)
    evens = ones(match) - odds
    most = jnp.maximum(jnp.sum(evens, axis=1, keepdims=True), jnp.sum(odds, axis=1, keepdims=True))
    held = (most.astype(jnp.int32) + 1) >> 1
    held = jnp.broadcast_to(held, (keys, 128)).astype(jnp.float32)
    upto = ones(iota(keys, keys, 1) <= iota(keys, keys, 0)).astype(jnp.bfloat16)
    ends = jnp.dot(upto, held.astype(jnp.bfloat16), preferred_element_type=jnp.float32)
    early = ends[row_tiles - 1 : row_tiles].astype(jnp.int32)
    early_steps = (early + UNROLL - 1) >> UNROLL.bit_length() - 1
    gap = (early_steps * UNROLL - early).astype(jnp.float32)
    ends = ends + jnp.where(iota(keys, 128, 0) < row_tiles, 0.0, gap)
    base = ends - held
    last_steps = (ends[keys - 1 :].astype(jnp.int32) + UNROLL - 1) >> UNROLL.bit_length() - 1
    steps[...] = jnp.where(iota(1, 128, 1) == 0, early_steps, last_steps)

    before = ones(iota(slots, slots, 0) < iota(slots, slots, 1)).astype(jnp.bfloat16)
    even_rank = jnp.dot(evens.astype(jnp.bfloat16), before, preferred_element_type=jnp.float32)
    odd_rank = jnp.dot(odds.astype(jnp.bfloat16), before, preferred_element_type=jnp.float32)
    spots = (evens + odds) * base[:, :1] * GROUP + (evens * even_rank + odds * odd_rank) * 2
    place = jnp.sum(spots, axis=0, keepdims=True).astype(jnp.int32) + odd
    place = jnp.where(alive, place, -1)

    n_spots = block.shape[1]
    taken = ones(place == iota(n_spots, slots, 0)).astype(jnp.bfloat16)
    line = iota(8, slots, 0)
    values = jnp.where(line == 0, slot // 2, jnp.where(line == 1, col, jnp.where(line == 2, 1, 0)))
    values = values.astype(jnp.float32).astype(jnp.bfloat16)
    found = lax.dot_general(
        values, taken, (((1,), (1,)), ((), ())), preferred_element_type=jnp.float32
    )
    block[...] = jnp.where(found[2:3] > 0.5, found[:1], float(slots // 2)).astype(jnp.int32)
    column[...] = found[1:2].astype(jnp.int32)
    n_groups = group_row.shape[1]
    passed = ones(ends[:, :1] <= iota(keys, n_groups, 1).astype(jnp.float32))
    row = jnp.sum(passed, axis=0, keepdims=True).astype(jnp.int32)
    row = jnp.where(row < row_tiles, row, row - row_tiles)
    group_row[...] = jnp.where(row < row_tiles, row, 0)


def plan(rows, cols, live, me, own, row_tiles):
    groups = (rows.shape[1] + 2 * row_tiles) // 2 + UNROLL - 1
    spots = (groups * GROUP + 127) // 128 * 128
    scalar = pl.BlockSpec(memory_space=pltpu.SMEM)
    vmem = pl.BlockSpec(memory_space=pltpu.VMEM)
    return pl.pallas_call(
        functools.partial(plan_kernel, own.shape[0] // TILE, row_tiles),
        out_shape=[jax.ShapeDtypeStruct((1, n), jnp.int32) for n in (spots, spots, 384, 128)]
        + [jax.ShapeDtypeStruct(own.shape, own.dtype)],
        in_specs=[scalar] * 2 + [pl.BlockSpec(memory_space=pl.ANY)] * 3,
        out_specs=[vmem] * 5,
        scratch_shapes=[pltpu.VMEM(rows.shape, jnp.int32)] * 2 + [pltpu.SemaphoreType.DMA((3,))],
        compiler_params=pltpu.CompilerParams(vmem_limit_bytes=40 << 20),
        name="plan",
    )(me, live, rows, cols, own)


def tile_copies(tiles_hbm, tiles, sems):
    chunk = tiles_hbm.shape[0] // CHUNKS
    return [
        pltpu.make_async_copy(
            tiles_hbm.at[pl.ds(i * chunk, chunk)], tiles.at[pl.ds(i * chunk, chunk)], sems.at[i]
        )
        for i in range(CHUNKS)
    ]


def fill_table(table, parts, weight):
    part_tiles, _, depth = parts[0].shape
    step = 8
    for i, part in enumerate(parts):

        def some(k, carry):
            rows = part[pl.ds(k * step, step)].reshape(step * TILE, depth)
            made = jnp.dot(rows, weight[...], preferred_element_type=jnp.float32)
            made = made.astype(table.dtype).reshape(step, TILE, table.shape[2])
            table[pl.ds(i * part_tiles + k * step, step)] = made
            return carry

        lax.fori_loop(0, part_tiles // step, some, 0)


def add_groups(first, last, block, column, group_row, tiles, table, total):
    left = lax.broadcasted_iota(jnp.int32, (TILE, 2 * TILE), 1) < TILE

    def step(i, carry):
        terms = []
        for j in range(UNROLL):
            spots = [(i * UNROLL + j) * GROUP + t for t in range(GROUP)]
            lhs = [
                jnp.where(left, tiles[block[0, spots[t]]], tiles[block[0, spots[t + 1]]])
                for t in range(0, GROUP, 2)
            ]
            rhs = [table[column[0, spot]] for spot in spots]
            terms.append(
                jnp.dot(
                    jnp.concatenate(lhs, axis=1),
                    jnp.concatenate(rhs, axis=0),
                    preferred_element_type=jnp.float32,
                )
            )
        for j in range(UNROLL):
            total[group_row[0, i * UNROLL + j]] += terms[j]
        return carry

    lax.fori_loop(first, last, step, 0)


def spmm_kernel(late, block, column, group_row, steps, *refs):
    if late:
        odd_z, weight, *parts, tiles_hbm, before = refs[:-7]
        kept, first_half, second_half, table, tiles, total, sems = refs[-7:]
    else:
        weight, *parts, tiles_hbm, total, table, tiles, sems = refs
    copies = tile_copies(tiles_hbm, tiles, sems)
    for copy in copies:
        copy.start()
    tiles[tiles_hbm.shape[0]] = jnp.zeros(tiles.shape[1:], tiles.dtype)
    total[...] = before[...] if late else jnp.zeros_like(total)
    fill_table(table, parts, weight)
    for copy in copies:
        copy.wait()
    first, last = (steps[0, 0], steps[0, 1]) if late else (0, steps[0, 0])
    add_groups(first, last, block, column, group_row, tiles, table, total)
    if late:
        n_pairs, per_pair, lanes = kept.shape[0], kept.shape[1], first_half.shape[3]
        for pair in range(n_pairs):
            here = total[pl.ds((2 * pair + odd_z[0]) * per_pair, per_pair)]
            there = total[pl.ds((2 * pair + 1 - odd_z[0]) * per_pair, per_pair)]
            kept[pair] = here
            first_half[pair] = there[:, :, :lanes].astype(first_half.dtype)
            second_half[pair] = there[:, :, lanes:].astype(second_half.dtype)


def spmm(plan, weight, parts, tiles, row_tiles, before=None, odd_z=None, n_pairs=None):
    width = weight.shape[1]
    scalar = pl.BlockSpec(memory_space=pltpu.SMEM)
    vmem = pl.BlockSpec(memory_space=pltpu.VMEM)
    anywhere = pl.BlockSpec(memory_space=pl.ANY)
    sums = (row_tiles, TILE, width)
    scratch = [
        pltpu.VMEM((len(parts) * parts[0].shape[0], TILE, width), jnp.bfloat16),
        pltpu.VMEM((tiles.shape[0] + 1, *tiles.shape[1:]), tiles.dtype),
    ]
    late = before is not None
    scalars = list(plan)
    if late:
        scalars.append(odd_z)
        scratch.append(pltpu.VMEM(sums, jnp.float32))
        out = (n_pairs, row_tiles // (2 * n_pairs), TILE)
        half = jax.ShapeDtypeStruct((*out, width // 2), jnp.bfloat16)
        outs = [jax.ShapeDtypeStruct((*out, width), jnp.float32), half, half]
    else:
        outs = jax.ShapeDtypeStruct(sums, jnp.float32)
    return pl.pallas_call(
        functools.partial(spmm_kernel, late),
        out_shape=outs,
        in_specs=[scalar] * len(scalars)
        + [vmem] * (1 + len(parts))
        + [anywhere]
        + [vmem] * late,
        out_specs=[vmem] * 3 if late else vmem,
        scratch_shapes=scratch + [pltpu.SemaphoreType.DMA((CHUNKS,))],
        compiler_params=pltpu.CompilerParams(vmem_limit_bytes=SPMM_VMEM),
        name="late_groups" if late else "early_groups",
    )(*scalars, weight, *parts, tiles, *([before] if late else []))


def merge_kernel(kept, first_half, second_half, out):
    lanes = first_half.shape[3]
    first = kept[:, :, :, :lanes] + first_half[...].astype(jnp.float32)
    second = kept[:, :, :, lanes:] + second_half[...].astype(jnp.float32)
    out[:, :, :, :lanes] = first.astype(out.dtype)
    out[:, :, :, lanes:] = second.astype(out.dtype)


def merge(kept, first_half, second_half):
    vmem = pl.BlockSpec(memory_space=pltpu.VMEM)
    return pl.pallas_call(
        merge_kernel,
        out_shape=jax.ShapeDtypeStruct(kept.shape, jnp.bfloat16),
        in_specs=[vmem] * 3,
        out_specs=vmem,
        compiler_params=pltpu.CompilerParams(vmem_limit_bytes=SPMM_VMEM),
        name="merge_pair",
    )(kept, first_half, second_half)


SPMM_VMEM = 46 << 20


def body(features, weight, tiles, tile_rows, tile_cols, counts):
    own, width = features.shape
    n_col = lax.axis_size("col")
    row_tiles = n_col * own // TILE
    me = lax.axis_index("row")
    my_y, my_x = me // (X_CHIPS * CORES), me // CORES % X_CHIPS

    def part(value):
        return both_cores(value).reshape(-1, TILE, width)

    pieces = [shift(features, k, 0) for k in (1, 2, 3)]
    place = jnp.stack([my_y, my_x]).astype(jnp.int32)
    *groups, own_rows = plan(tile_rows[0], tile_cols[0], counts, place, features, row_tiles)
    *pieces, block, column, group_row, steps = lax.optimization_barrier(
        (own_rows, *pieces, *groups)
    )
    line = jnp.concatenate(pieces, axis=0)
    across = shift(line, 0, 2)
    own_line, line = lax.optimization_barrier((part(line), line))
    behind, ahead = shift(line, 0, 1), shift(line, 0, 3)

    groups = (block, column, group_row, steps)
    early = spmm(groups, weight, [own_line, part(across)], tiles[0, 0], row_tiles)
    early, ahead = lax.optimization_barrier((early, ahead))
    late_parts = [part(ahead), part(behind)]
    z = lax.axis_index("col") // HALVES
    odd_z = (z % 2).reshape(1).astype(jnp.int32)
    n_pairs = n_col // (2 * HALVES)
    kept, first_half, second_half = spmm(
        groups, weight, late_parts, tiles[0, 0], row_tiles, early, odd_z, n_pairs
    )
    first_half = lax.ppermute(first_half, "col", z_neighbours(n_col, 0))
    second_half = lax.ppermute(second_half, "col", z_neighbours(n_col, 1))
    sums = merge(kept, first_half, second_half).reshape(-1, width)

    groups = [
        [(2 * pair + odd) * HALVES + half for pair in range(n_pairs) for half in range(HALVES)]
        for odd in range(2)
    ]
    received = lax.all_to_all(sums, "col", 0, 0, axis_index_groups=groups, tiled=True)
    received = received.reshape(len(groups[0]), own, width).astype(jnp.float32)
    return jnp.maximum(jnp.sum(received, axis=0), 0.0).astype(jnp.bfloat16)


def solution(mesh):
    return jax.shard_map(
        body,
        mesh=mesh,
        in_specs=(
            P(("row", "col"), None),
            P(),
            P("row", "col", None, None, None),
            P("row", "col", None),
            P("row", "col", None),
            P("row", "col"),
        ),
        out_specs=P(("row", "col"), None),
        check_vma=False,
    )
```

```python
import functools

import jax
import jax.numpy as jnp
from jax import lax
from jax.experimental import pallas as pl
from jax.experimental.pallas import tpu as pltpu
from jax.sharding import PartitionSpec as P

TILE = 64
Y_CHIPS, X_CHIPS, CORES = 4, 4, 2
HALVES = 2
GROUP = 4
UNROLL = 16
CHUNKS = 4


def shift(value, dy, dx):
    pairs = []
    for source in range(Y_CHIPS * X_CHIPS * CORES):
        y, x, core = source // (X_CHIPS * CORES), source // CORES % X_CHIPS, source % CORES
        y, x = (y + dy) % Y_CHIPS, (x + dx) % X_CHIPS
        pairs.append((source, (y * X_CHIPS + x) * CORES + core))
    return lax.ppermute(value, "row", pairs)


def z_neighbours(n_col, offset):
    n_z = n_col // HALVES
    pairs = []
    for source in range(n_col):
        z, half = source // HALVES, source % HALVES
        z = (z + 1 if z % 2 == offset else z - 1) % n_z
        pairs.append((source, z * HALVES + half))
    return pairs


def both_cores(value):
    groups = [[2 * chip, 2 * chip + 1] for chip in range(Y_CHIPS * X_CHIPS)]
    return lax.all_gather(value, "row", axis_index_groups=groups, axis=0, tiled=True)


def plan_kernel(own_tiles, row_tiles, me, live, rows_hbm, cols_hbm, own_hbm, *refs):
    block, column, group_row, steps, own, rows_ref, cols_ref, sems = refs
    copies = [
        pltpu.make_async_copy(source, target, sems.at[i])
        for i, (source, target) in enumerate(
            ((rows_hbm, rows_ref), (cols_hbm, cols_ref), (own_hbm, own))
        )
    ]
    for copy in copies:
        copy.start()
    for copy in copies:
        copy.wait()
    slots = rows_ref.shape[1]
    keys = 2 * row_tiles

    def iota(rows, lanes, axis):
        return lax.broadcasted_iota(jnp.int32, (rows, lanes), axis)

    def ones(mask):
        return jnp.where(mask, 1.0, 0.0)

    slot = iota(1, slots, 1)
    odd = slot & 1
    alive = slot < live[0, 0]
    owner = (cols_ref[...] * (128 // own_tiles + 1)) >> 7
    inner = cols_ref[...] - owner * own_tiles
    y, x, core = owner // (X_CHIPS * CORES), owner // CORES % X_CHIPS, owner % CORES
    back_y, back_x = (me[0] - y) % Y_CHIPS, (me[1] - x) % X_CHIPS
    late = back_x % 2
    col = ((back_x // 2 ^ late) * CORES + core) * Y_CHIPS * own_tiles + back_y * own_tiles + inner
    key = jnp.where(alive, late * row_tiles + rows_ref[...], keys)

    match = key == iota(keys, slots, 0)
    is_odd = jnp.broadcast_to(odd, (keys, slots)) == 1
    odds = ones(match & is_odd)
    evens = ones(match) - odds
    most = jnp.maximum(jnp.sum(evens, axis=1, keepdims=True), jnp.sum(odds, axis=1, keepdims=True))
    held = (most.astype(jnp.int32) + 1) >> 1
    held = jnp.broadcast_to(held, (keys, 128)).astype(jnp.float32)
    upto = ones(iota(keys, keys, 1) <= iota(keys, keys, 0)).astype(jnp.bfloat16)
    ends = jnp.dot(upto, held.astype(jnp.bfloat16), preferred_element_type=jnp.float32)
    early = ends[row_tiles - 1 : row_tiles].astype(jnp.int32)
    early_steps = (early + UNROLL - 1) >> UNROLL.bit_length() - 1
    gap = (early_steps * UNROLL - early).astype(jnp.float32)
    ends = ends + jnp.where(iota(keys, 128, 0) < row_tiles, 0.0, gap)
    base = ends - held
    last_steps = (ends[keys - 1 :].astype(jnp.int32) + UNROLL - 1) >> UNROLL.bit_length() - 1
    steps[...] = jnp.where(iota(1, 128, 1) == 0, early_steps, last_steps)

    before = ones(iota(slots, slots, 0) < iota(slots, slots, 1)).astype(jnp.bfloat16)
    even_rank = jnp.dot(evens.astype(jnp.bfloat16), before, preferred_element_type=jnp.float32)
    odd_rank = jnp.dot(odds.astype(jnp.bfloat16), before, preferred_element_type=jnp.float32)
    spots = (evens + odds) * base[:, :1] * GROUP + (evens * even_rank + odds * odd_rank) * 2
    place = jnp.sum(spots, axis=0, keepdims=True).astype(jnp.int32) + odd
    place = jnp.where(alive, place, -1)

    n_spots = block.shape[1]
    taken = ones(place == iota(n_spots, slots, 0)).astype(jnp.bfloat16)
    line = iota(8, slots, 0)
    values = jnp.where(line == 0, slot // 2, jnp.where(line == 1, col, jnp.where(line == 2, 1, 0)))
    values = values.astype(jnp.float32).astype(jnp.bfloat16)
    found = lax.dot_general(
        values, taken, (((1,), (1,)), ((), ())), preferred_element_type=jnp.float32
    )
    block[...] = found[:1].astype(jnp.int32)
    empty = float(own_tiles * Y_CHIPS * CORES * 2)
    column[...] = jnp.where(found[2:3] > 0.5, found[1:2], empty).astype(jnp.int32)
    n_groups = group_row.shape[1]
    passed = ones(ends[:, :1] <= iota(keys, n_groups, 1).astype(jnp.float32))
    row = jnp.sum(passed, axis=0, keepdims=True).astype(jnp.int32)
    row = jnp.where(row < row_tiles, row, row - row_tiles)
    group_row[...] = jnp.where(row < row_tiles, row, 0)


def plan(rows, cols, live, me, own, row_tiles):
    groups = (rows.shape[1] + 2 * row_tiles) // 2 + UNROLL - 1
    spots = (groups * GROUP + 127) // 128 * 128
    scalar = pl.BlockSpec(memory_space=pltpu.SMEM)
    vmem = pl.BlockSpec(memory_space=pltpu.VMEM)
    return pl.pallas_call(
        functools.partial(plan_kernel, own.shape[0] // TILE, row_tiles),
        out_shape=[jax.ShapeDtypeStruct((1, n), jnp.int32) for n in (spots, spots, 384, 128)]
        + [jax.ShapeDtypeStruct(own.shape, own.dtype)],
        in_specs=[scalar] * 2 + [pl.BlockSpec(memory_space=pl.ANY)] * 3,
        out_specs=[vmem] * 5,
        scratch_shapes=[pltpu.VMEM(rows.shape, jnp.int32)] * 2 + [pltpu.SemaphoreType.DMA((3,))],
        compiler_params=pltpu.CompilerParams(vmem_limit_bytes=40 << 20),
        name="plan",
    )(me, live, rows, cols, own)


def tile_copies(tiles_hbm, tiles, sems):
    chunk = tiles_hbm.shape[0] // CHUNKS
    return [
        pltpu.make_async_copy(
            tiles_hbm.at[pl.ds(i * chunk, chunk)], tiles.at[pl.ds(i * chunk, chunk)], sems.at[i]
        )
        for i in range(CHUNKS)
    ]


def fill_table(table, parts, weight):
    part_tiles, _, depth = parts[0].shape
    step = 8
    for i, part in enumerate(parts):

        def some(k, carry):
            rows = part[pl.ds(k * step, step)].reshape(step * TILE, depth)
            made = jnp.dot(rows, weight[...], preferred_element_type=jnp.float32)
            made = made.astype(table.dtype).reshape(step, TILE, table.shape[2])
            table[pl.ds(i * part_tiles + k * step, step)] = made
            return carry

        lax.fori_loop(0, part_tiles // step, some, 0)


def add_groups(first, last, block, column, group_row, tiles, table, total):
    left = lax.broadcasted_iota(jnp.int32, (TILE, 2 * TILE), 1) < TILE

    def step(i, carry):
        terms = []
        for j in range(UNROLL):
            spots = [(i * UNROLL + j) * GROUP + t for t in range(GROUP)]
            lhs = [
                jnp.where(left, tiles[block[0, spots[t]]], tiles[block[0, spots[t + 1]]])
                for t in range(0, GROUP, 2)
            ]
            rhs = [table[column[0, spot]] for spot in spots]
            terms.append(
                jnp.dot(
                    jnp.concatenate(lhs, axis=1),
                    jnp.concatenate(rhs, axis=0),
                    preferred_element_type=jnp.float32,
                )
            )
        for j in range(UNROLL):
            total[group_row[0, i * UNROLL + j]] += terms[j]
        return carry

    lax.fori_loop(first, last, step, 0)


def spmm_kernel(late, block, column, group_row, steps, *refs):
    if late:
        odd_z, weight, *parts, tiles, before = refs[:-5]
        kept, first_half, second_half, table, total = refs[-5:]
        copies = []
    else:
        weight, *parts, tiles_hbm, total, table, tiles, sems = refs
        copies = tile_copies(tiles_hbm, tiles, sems)
    for copy in copies:
        copy.start()
    total[...] = before[...] if late else jnp.zeros_like(total)
    fill_table(table, parts, weight)
    last_tile = table.shape[0] - 1
    table[last_tile] = jnp.zeros(table.shape[1:], table.dtype)
    for copy in copies:
        copy.wait()
    first, last = (steps[0, 0], steps[0, 1]) if late else (0, steps[0, 0])
    add_groups(first, last, block, column, group_row, tiles, table, total)
    if late:
        n_pairs, per_pair, lanes = kept.shape[0], kept.shape[1], first_half.shape[3]
        for pair in range(n_pairs):
            here = total[pl.ds((2 * pair + odd_z[0]) * per_pair, per_pair)]
            there = total[pl.ds((2 * pair + 1 - odd_z[0]) * per_pair, per_pair)]
            kept[pair] = here
            first_half[pair] = there[:, :, :lanes].astype(first_half.dtype)
            second_half[pair] = there[:, :, lanes:].astype(second_half.dtype)


def spmm(plan, weight, parts, tiles, row_tiles, before=None, odd_z=None, n_pairs=None):
    width = weight.shape[1]
    scalar = pl.BlockSpec(memory_space=pltpu.SMEM)
    vmem = pl.BlockSpec(memory_space=pltpu.VMEM)
    anywhere = pl.BlockSpec(memory_space=pl.ANY)
    sums = (row_tiles, TILE, width)
    scratch = [pltpu.VMEM((len(parts) * parts[0].shape[0] + 1, TILE, width), jnp.bfloat16)]
    late = before is not None
    scalars = list(plan)
    if late:
        scalars.append(odd_z)
        scratch.append(pltpu.VMEM(sums, jnp.float32))
        out = (n_pairs, row_tiles // (2 * n_pairs), TILE)
        half = jax.ShapeDtypeStruct((*out, width // 2), jnp.bfloat16)
        outs = [jax.ShapeDtypeStruct((*out, width), jnp.float32), half, half]
    else:
        scratch += [pltpu.VMEM(tiles.shape, tiles.dtype), pltpu.SemaphoreType.DMA((CHUNKS,))]
        outs = jax.ShapeDtypeStruct(sums, jnp.float32)
    return pl.pallas_call(
        functools.partial(spmm_kernel, late),
        out_shape=outs,
        in_specs=[scalar] * len(scalars)
        + [vmem] * (1 + len(parts))
        + ([vmem] * 2 if late else [anywhere]),
        out_specs=[vmem] * 3 if late else vmem,
        scratch_shapes=scratch,
        compiler_params=pltpu.CompilerParams(vmem_limit_bytes=LATE_VMEM if late else SPMM_VMEM),
        name="late_groups" if late else "early_groups",
    )(*scalars, weight, *parts, tiles, *([before] if late else []))


def merge_kernel(kept, first_half, second_half, out):
    lanes = first_half.shape[3]
    first = kept[:, :, :, :lanes] + first_half[...].astype(jnp.float32)
    second = kept[:, :, :, lanes:] + second_half[...].astype(jnp.float32)
    out[:, :, :, :lanes] = first.astype(out.dtype)
    out[:, :, :, lanes:] = second.astype(out.dtype)


def merge(kept, first_half, second_half):
    vmem = pl.BlockSpec(memory_space=pltpu.VMEM)
    return pl.pallas_call(
        merge_kernel,
        out_shape=jax.ShapeDtypeStruct(kept.shape, jnp.bfloat16),
        in_specs=[vmem] * 3,
        out_specs=vmem,
        compiler_params=pltpu.CompilerParams(vmem_limit_bytes=SPMM_VMEM),
        name="merge_pair",
    )(kept, first_half, second_half)


SPMM_VMEM = 46 << 20
LATE_VMEM = 24 << 20


def body(features, weight, tiles, tile_rows, tile_cols, counts):
    own, width = features.shape
    n_col = lax.axis_size("col")
    row_tiles = n_col * own // TILE
    me = lax.axis_index("row")
    my_y, my_x = me // (X_CHIPS * CORES), me // CORES % X_CHIPS

    def part(value):
        return both_cores(value).reshape(-1, TILE, width)

    pieces = [shift(features, k, 0) for k in (1, 2, 3)]
    place = jnp.stack([my_y, my_x]).astype(jnp.int32)
    *groups, own_rows = plan(tile_rows[0], tile_cols[0], counts, place, features, row_tiles)
    *pieces, block, column, group_row, steps = lax.optimization_barrier(
        (own_rows, *pieces, *groups)
    )
    line = jnp.concatenate(pieces, axis=0)
    across = shift(line, 0, 2)
    own_line, line = lax.optimization_barrier((part(line), line))
    behind, ahead = shift(line, 0, 1), shift(line, 0, 3)

    groups = (block, column, group_row, steps)
    early = spmm(groups, weight, [own_line, part(across)], tiles[0, 0], row_tiles)
    early, ahead = lax.optimization_barrier((early, ahead))
    late_parts = [part(ahead), part(behind)]
    z = lax.axis_index("col") // HALVES
    odd_z = (z % 2).reshape(1).astype(jnp.int32)
    n_pairs = n_col // (2 * HALVES)
    kept, first_half, second_half = spmm(
        groups, weight, late_parts, tiles[0, 0], row_tiles, early, odd_z, n_pairs
    )
    first_half = lax.ppermute(first_half, "col", z_neighbours(n_col, 0))
    second_half = lax.ppermute(second_half, "col", z_neighbours(n_col, 1))
    sums = merge(kept, first_half, second_half).reshape(-1, width)

    groups = [
        [(2 * pair + odd) * HALVES + half for pair in range(n_pairs) for half in range(HALVES)]
        for odd in range(2)
    ]
    received = lax.all_to_all(sums, "col", 0, 0, axis_index_groups=groups, tiled=True)
    received = received.reshape(len(groups[0]), own, width).astype(jnp.float32)
    return jnp.maximum(jnp.sum(received, axis=0), 0.0).astype(jnp.bfloat16)


def solution(mesh):
    return jax.shard_map(
        body,
        mesh=mesh,
        in_specs=(
            P(("row", "col"), None),
            P(),
            P("row", "col", None, None, None),
            P("row", "col", None),
            P("row", "col", None),
            P("row", "col"),
        ),
        out_specs=P(("row", "col"), None),
        check_vma=False,
    )
```
